128 devices in a mesh: energy: 4 (over z), cols: 32 (over x, y, core).
Axes of the slice: x: 4, y: 4, z: 4, core: 2. Of those that a mesh axis runs over, the one named last changes fastest.
Arguments:
- left_inverse: bfloat16 [12, 2, 1536, 1536], P('energy', None, 'cols'), parts along dimension 0, as said below
- regions: int32 [3, 1536], replicated, may hold values from 0 to 2
- region_mass: float32 [3], replicated, may hold values from 1 to 2.5
- region_alpha: float32 [3], replicated, may hold values from 0.1 to 0.5
- energy_grid: float32 [16], replicated, may hold values from 0.2 to 1
- energy_index: int32 [4], P('energy'), parts along dimension 0, may hold values from 0 to 15
Outputs:
- green: float32 [8, 2, 1536, 1536], P('energy', None, 'cols'), parts along dimension 0
The draws below stay inside these ranges and needn't reach their ends.
There are 4 independent parts, one for each index of `energy`. The reference program is written for one: setup_inputs(seed, part) draws one part's arguments, and reference() takes and returns one part's arrays. A program takes and returns all parts, laid end to end along the dimension named above; an argument that names none is the same for every part. Nothing has to cross between parts.
Inputs may be any that keep to these rules, and one draw needn't show every extreme that they name: Every block of left_inverse is complex symmetric: both planes equal their transposes.
All inputs are finite; a program needn't handle non-finite values.
Results may differ from the reference program's by a relative error of at most 0.0024.
Values may be sent and summed in bfloat16 or wider, within the bound.
A program may use at most 128 MiB of HBM per device.

```python
import math
import jax
import jax.numpy as jnp

P_SIZE = 1536
SLICES = 3
REGIONS = 3
NE = 16


def draw_left_inverse(key, part):
    keys = jax.random.split(jax.random.fold_in(key, 7), 3)
    shape = (SLICES, 2, P_SIZE, P_SIZE)
    noise = jax.random.normal(keys[0], shape, jnp.float32)
    noise = noise * (0.6 / P_SIZE ** 0.5)
    symmetric = (noise + jnp.swapaxes(noise, 2, 3)) * 0.70710678
    real_diag = jax.random.uniform(keys[1], (SLICES, 1, P_SIZE), jnp.float32, 0.5, 1.2)
    imag_diag = jax.random.uniform(keys[2], (SLICES, 1, P_SIZE), jnp.float32, -0.8, -0.2)
    diagonal = jnp.concatenate([real_diag, imag_diag], axis=1)
    identity = jnp.eye(P_SIZE, dtype=jnp.float32)
    block = symmetric * (1.0 - identity) + identity * diagonal[:, :, :, None]
    return block.astype(jnp.bfloat16)


def touch_ends(values, own_key, smallest, top_value):
    longest = values.shape.index(max(values.shape))
    spots = []
    for shift in (0, 1):
        where = [jax.random.randint(jax.random.fold_in(own_key, axis), (), 0, length) for axis, length in enumerate(values.shape)]
        where[longest] = (where[longest] + shift) % values.shape[longest]
        spots.append(tuple(where))
    return values.at[spots[0]].set(smallest).at[spots[1]].set(top_value)


def setup_inputs(seed: int = 0, part: int = 0) -> dict:
    streams_of = jax.random.split(jax.random.key(seed), 7)
    part_splits = jax.random.split(jax.random.fold_in(streams_of[6], part), 7)
    left_inverse = draw_left_inverse(jax.random.fold_in(jax.random.fold_in(streams_of[6], part), 71), part)
    regions = touch_ends(jax.random.randint(streams_of[1], (SLICES, P_SIZE), 0, REGIONS), jax.random.fold_in(streams_of[1], 1), 0, REGIONS - 1).astype(jnp.int32)
    region_mass = jnp.clip(jnp.exp(jax.random.uniform(streams_of[2], (REGIONS,), jnp.float32, math.log(1.0), math.log(2.5))), 1.0, 2.5)
    region_alpha = jnp.clip(jnp.exp(jax.random.uniform(streams_of[3], (REGIONS,), jnp.float32, math.log(0.1), math.log(0.5))), 0.1, 0.5)
    energy_grid = jnp.clip(jax.random.uniform(streams_of[4], (NE,), jnp.float32, 0.2, 1.0), 0.2, 1.0)
    energy_index = jax.random.randint(part_splits[5], (1,), 0, NE).astype(jnp.int32)
    return {"left_inverse": left_inverse, "regions": regions, "region_mass": region_mass, "region_alpha": region_alpha, "energy_grid": energy_grid, "energy_index": energy_index}


def complex_product(left, right):
    real = jnp.dot(left[0], right[0], preferred_element_type=jnp.float32) - jnp.dot(left[1], right[1], preferred_element_type=jnp.float32)
    imag = jnp.dot(left[0], right[1], preferred_element_type=jnp.float32) + jnp.dot(left[1], right[0], preferred_element_type=jnp.float32)
    return jnp.stack([real, imag])


def couplings(regions, region_mass, region_alpha, energy_grid, energy_index):
    level = jnp.sum(jnp.where(jnp.arange(energy_grid.shape[0]) == energy_index[0], energy_grid, 0.0))
    onehot = (regions[:, :, None] == jnp.arange(region_mass.shape[0])[None, None, :]).astype(jnp.float32)
    per_region = region_mass * (1.0 + region_alpha * level)
    mass = jnp.sum(onehot * per_region[None, None, :], axis=2)
    return 2.0 / (mass[:-1] + mass[1:])


def reference(left_inverse, regions, region_mass, region_alpha, energy_grid, energy_index):
    hop = couplings(regions, region_mass, region_alpha, energy_grid, energy_index)
    count = left_inverse.shape[0]
    next_green = left_inverse[count - 1]
    blocks = []
    for index in range(count - 2, -1, -1):
        panel = left_inverse[index]
        factor = hop[index][None, :, None]
        scaled = (factor * panel.astype(jnp.float32)).astype(jnp.bfloat16)
        image = (factor * complex_product(next_green, scaled)).astype(jnp.bfloat16)
        current = panel.astype(jnp.float32) + complex_product(panel, image)
        blocks.append(current)
        next_green = current.astype(jnp.bfloat16)
    return jnp.stack(blocks[::-1])
```

```python
import functools

import jax
import jax.numpy as jnp
from jax import lax
from jax.experimental import pallas as pl
from jax.experimental.pallas import tpu as pltpu
from jax.sharding import PartitionSpec as P

SIDE = 4
CORES = 2
BF = jnp.bfloat16
F32 = jnp.float32


def dot(a, b):
    return lax.dot_general(a, b, (((1,), (0,)), ((), ())), preferred_element_type=F32)


def dot_t(a, b):
    return lax.dot_general(a, b, (((1,), (1,)), ((), ())), preferred_element_type=F32)


def complex_dot(ar, ai, br, bi, op):
    return op(ar, br) - op(ai, bi), op(ar, bi) + op(ai, br)


class Sems:
    def __init__(self, ref):
        self.ref = ref
        self.used = 0

    def take(self):
        self.used += 1
        return self.ref.at[self.used - 1]


class Gather:
    def __init__(self, me, device, source, slot, send, recv, sibling=None):
        self.me = me
        self.plus = lax.rem(me + 1, SIDE)
        self.minus = lax.rem(me + 3, SIDE)
        self.far = lax.rem(me + 2, SIDE)
        self.device, self.source, self.slot = device, source, slot
        self.send, self.recv = send, recv
        self.sibling = sibling
        self.copies = []
        self.sib = {}

    def remote(self, src, dst, device):
        copy = pltpu.make_async_remote_copy(
            src_ref=src,
            dst_ref=dst,
            send_sem=self.send.take(),
            recv_sem=self.recv.take(),
            device_id={"cols": device},
            device_id_type=pl.DeviceIdType.MESH,
        )
        copy.start()
        self.copies.append(copy)
        return copy

    def start(self):
        right, left = self.device(self.plus), self.device(self.minus)
        me = self.me
        self.r0 = self.remote(self.source(0), self.slot(me, 0), right)
        self.l1 = self.remote(self.source(1), self.slot(me, 1), left)
        self.r1 = self.remote(self.source(1), self.slot(me, 1), right)
        self.l0 = self.remote(self.source(0), self.slot(me, 0), left)
        if self.sibling is not None:
            for p in range(2):
                self.share("own", me, p, self.source(p))

    def share(self, name, slot, p, src=None):
        if self.sibling is None:
            return
        ref = self.slot(slot, p)
        self.sib[name, p] = self.remote(ref if src is None else src, ref, self.sibling)

    def forward(self):
        self.r0.wait_recv()
        self.fr = self.remote(self.slot(self.minus, 0), self.slot(self.minus, 0), self.device(self.plus))
        self.l1.wait_recv()
        self.fl = self.remote(self.slot(self.plus, 1), self.slot(self.plus, 1), self.device(self.minus))
        self.share("minus", self.minus, 0)
        self.share("plus", self.plus, 1)

    def near(self):
        self.r1.wait_recv()
        self.share("minus", self.minus, 1)
        self.l0.wait_recv()
        self.share("plus", self.plus, 0)

    def last(self):
        self.fr.wait_recv()
        self.share("far", self.far, 0)
        self.fl.wait_recv()
        self.share("far", self.far, 1)

    def sib_wait(self, name):
        if self.sibling is not None:
            for p in range(2):
                self.sib[name, p].wait_recv()

    def drain(self):
        for copy in self.copies:
            copy.wait_send()


def group_order(pieces):
    return jnp.concatenate([pieces[b][a] for a in range(SIDE) for b in range(SIDE)], axis=-1)


def exchanged(value, width):
    rows = [
        [value[:, (a * SIDE + b) * width : (a * SIDE + b + 1) * width] for b in range(SIDE)] for a in range(SIDE)
    ]
    return group_order(rows)


def kernel(
    left,
    regions,
    region_mass,
    region_alpha,
    energy_grid,
    energy_index,
    out,
    row2,
    row1,
    row0,
    col1,
    col0,
    scaled,
    mine0,
    image1,
    image0,
    green1,
    final,
    ends,
    acc,
    hop_t,
    pick,
    send_sems,
    recv_sems,
    local_sems,
):
    me = lax.axis_index("cols")
    c = lax.rem(me, CORES)
    j = lax.rem(me // CORES, SIDE)
    i = me // (CORES * SIDE)
    sibling = me + 1 - 2 * c

    def at(x, y):
        return (x * SIDE + y) * CORES + c

    def along_x(x):
        return at(x, j)

    def along_y(y):
        return at(i, y)

    rows = left.shape[2]
    size = left.shape[3]
    chip = CORES * rows
    panel = SIDE * chip
    high = SIDE * rows

    send, recv, local = Sems(send_sems), Sems(recv_sems), Sems(local_sems)

    barrier = pltpu.get_barrier_semaphore()
    peers = [sibling] + [along_x(lax.rem(i + s, SIDE)) for s in (1, 3)] + [along_y(lax.rem(j + s, SIDE)) for s in (1, 2, 3)]
    for peer in peers:
        pl.semaphore_signal(barrier, inc=1, device_id={"cols": peer}, device_id_type=pl.DeviceIdType.MESH)
    pl.semaphore_wait(barrier, len(peers))

    g_row2 = Gather(j, along_y, lambda p: left.at[2, p], lambda s, p: row2.at[p, s], send, recv)
    g_col1 = Gather(i, along_x, lambda p: left.at[1, p], lambda s, p: col1.at[p, s, c], send, recv, sibling)
    g_row1 = Gather(j, along_y, lambda p: left.at[1, p], lambda s, p: row1.at[p, s], send, recv)
    g_image1 = Gather(
        i, along_x, lambda p: image1.at[p, i, :, c], lambda s, p: image1.at[p, s, :, c], send, recv, sibling
    )
    g_green = Gather(j, along_y, lambda p: green1.at[p, j], lambda s, p: green1.at[p, s], send, recv)
    g_col0 = Gather(i, along_x, lambda p: mine0.at[p], lambda s, p: col0.at[p, s, c], send, recv, sibling)
    g_row0 = Gather(j, along_y, lambda p: left.at[0, p], lambda s, p: row0.at[p, s], send, recv)
    g_image0 = Gather(
        i, along_x, lambda p: image0.at[p, i, :, c], lambda s, p: image0.at[p, s, :, c], send, recv, sibling
    )

    g_row2.start()
    g_col1.start()
    locals_ = {}
    for name, src, dst in (
        ("row2", 2, lambda p: row2.at[p, j]),
        ("col1", 1, lambda p: col1.at[p, i, c]),
        ("row1", 1, lambda p: row1.at[p, j]),
        ("row0", 0, lambda p: row0.at[p, j]),
    ):
        locals_[name] = []
        for p in range(2):
            copy = pltpu.make_async_copy(left.at[src, p], dst(p), local.take())
            copy.start()
            locals_[name].append(copy)

    def local_wait(name):
        for copy in locals_[name]:
            copy.wait()

    level = jnp.float32(0.0)
    wanted = energy_index[0]
    for e in range(energy_grid.shape[0]):
        level = jnp.where(wanted == e, energy_grid[e], level)
    where = regions[...]
    mass = jnp.zeros(where.shape, F32)
    for r in range(region_mass.shape[0]):
        mass = jnp.where(where == r, region_mass[r] * (1.0 + region_alpha[r] * level), mass)
    hop0 = 2.0 / (mass[0:1] + mass[1:2])
    hop1 = 2.0 / (mass[1:2] + mass[2:3])
    for s, hop in enumerate((hop0, hop1)):
        for b in range(size // 128):
            tile = jnp.broadcast_to(hop[:, b * 128 : (b + 1) * 128], (128, 128))
            hop_t[s, b * 128 : (b + 1) * 128, :] = tile.T
    hop0_c = exchanged(hop0, chip)

    local_wait("row0")
    for p in range(2):
        mine0[p] = exchanged(row0[p, j].astype(F32), chip).astype(BF)

    for k in range(SIDE):
        n = lax.broadcasted_iota(jnp.int32, (panel, panel), 0)
        q = lax.broadcasted_iota(jnp.int32, (panel, panel), 1)
        keep = n + (k - j) * chip == q
        keep = keep & (q >= k * chip) & (q < (k + 1) * chip)
        pick[k * panel : (k + 1) * panel, :] = jnp.where(keep, 1.0, 0.0).astype(BF)

    def scale_block(col, slot, core, hop):
        for p in range(2):
            start = pl.multiple_of((slot * CORES + core) * rows, 16)
            scaled[p, pl.ds(start, rows), :] = (col[p, slot, core].astype(F32) * hop).astype(BF)

    def scale_own(col, slot, hop):
        scale_block(col, slot, c, hop)

    def scale_sib(g, name, col, slot, hop):
        g.sib_wait(name)
        scale_block(col, slot, 1 - c, hop)

    def store_image(image, s, real, imag):
        for m in range(SIDE):
            start = pl.multiple_of(i * panel + m * chip + c * rows, 16)
            h = hop_t[s, pl.ds(start, rows), :]
            h = jnp.concatenate([h] * (panel // 128), axis=1)
            part = slice(m * rows, (m + 1) * rows)
            image[0, i, m, c] = (h * real[part]).astype(BF)
            image[1, i, m, c] = (h * imag[part]).astype(BF)

    def init_acc(row):
        for p in range(2):
            acc[p] = dot(row[p].reshape(high, size), pick[...])

    def add_chunk(row, image, k):
        lanes = pl.ds(pl.multiple_of(k * panel, 128), panel)
        ar, ai = (row[p, :, :, lanes].reshape(high, panel) for p in range(2))
        br, bi = (image[p, k].reshape(panel, panel) for p in range(2))
        real, imag = complex_dot(ar, ai, br, bi, dot)
        acc[0] += real
        acc[1] += imag

    g_row2.forward()
    g_col1.forward()
    g_row1.start()
    local_wait("col1")
    scale_own(col1, i, hop1)
    scale_sib(g_col1, "own", col1, i, hop1)
    g_col1.near()
    g_row2.near()
    scale_own(col1, g_col1.minus, hop1)
    scale_own(col1, g_col1.plus, hop1)
    scale_sib(g_col1, "minus", col1, g_col1.minus, hop1)
    scale_sib(g_col1, "plus", col1, g_col1.plus, hop1)
    local_wait("row2")
    g_col1.last()
    g_row2.last()
    scale_own(col1, g_col1.far, hop1)
    scale_sib(g_col1, "far", col1, g_col1.far, hop1)

    ar, ai = (row2[p].reshape(high, size) for p in range(2))
    real, imag = complex_dot(ar, ai, scaled[0], scaled[1], dot_t)
    store_image(image1, 1, real, imag)
    g_image1.start()

    g_row1.forward()
    local_wait("row1")
    g_row1.near()
    g_image1.forward()
    g_col0.start()
    g_image1.near()
    g_row1.last()
    init_acc(row1)
    g_image1.sib_wait("own")
    add_chunk(row1, image1, i)
    for name, slot in (("minus", g_image1.minus), ("plus", g_image1.plus)):
        g_image1.sib_wait(name)
        add_chunk(row1, image1, slot)
    g_image1.last()
    g_image1.sib_wait("far")
    add_chunk(row1, image1, g_image1.far)
    for p in range(2):
        green1[p, j] = acc[p].astype(BF)
    g_green.start()

    g_col0.forward()
    g_col0.near()
    g_green.forward()
    g_row0.start()

    def scale_col0(name, slot):
        if name != "own":
            scale_own(col0, slot, hop0_c)
        scale_sib(g_col0, name, col0, slot, hop0_c)

    for p in range(2):
        start = pl.multiple_of((i * CORES + c) * rows, 16)
        scaled[p, pl.ds(start, rows), :] = (mine0[p].astype(F32) * hop0_c).astype(BF)
    scale_col0("own", i)
    scale_col0("minus", g_col0.minus)
    scale_col0("plus", g_col0.plus)
    g_col0.last()
    scale_col0("far", g_col0.far)

    def green_chunk(m, first=False):
        lanes = pl.ds(pl.multiple_of(m * panel, 128), panel)
        real, imag = complex_dot(green1[0, m], green1[1, m], scaled[0, :, lanes], scaled[1, :, lanes], dot_t)
        if first:
            acc[0] = real
            acc[1] = imag
        else:
            acc[0] += real
            acc[1] += imag

    green_chunk(j, True)
    g_green.near()
    green_chunk(g_green.minus)
    green_chunk(g_green.plus)
    g_green.last()
    green_chunk(g_green.far)
    store_image(image0, 0, acc[0], acc[1])
    g_image0.start()

    g_row0.forward()
    mine = pl.ds(pl.multiple_of(j * rows, 16), rows)
    for p in range(2):
        whole = jnp.concatenate([green1[p, m, mine, :].astype(F32) for m in range(SIDE)], axis=1)
        out[1, p] = exchanged(whole, chip)
    g_row0.near()
    g_image0.forward()
    g_image0.near()
    g_row0.last()
    init_acc(row0)
    g_image0.sib_wait("own")
    add_chunk(row0, image0, i)
    for name, slot in (("minus", g_image0.minus), ("plus", g_image0.plus)):
        g_image0.sib_wait(name)
        add_chunk(row0, image0, slot)
    g_image0.last()
    g_image0.sib_wait("far")
    add_chunk(row0, image0, g_image0.far)

    for m in range(SIDE):
        for p in range(2):
            ends[m, p] = acc[p, m * rows : (m + 1) * rows, :].astype(BF)
    tail = []
    for shift in (2, 1, 3):
        to = lax.rem(j + shift, SIDE)
        copy = pltpu.make_async_remote_copy(
            src_ref=ends.at[to],
            dst_ref=final.at[j],
            send_sem=send.take(),
            recv_sem=recv.take(),
            device_id={"cols": along_y(to)},
            device_id_type=pl.DeviceIdType.MESH,
        )
        copy.start()
        tail.append(copy)
    final[j] = ends[j]
    for copy in tail:
        copy.wait_recv()
    for p in range(2):
        whole = jnp.concatenate([final[m, p].astype(F32) for m in range(SIDE)], axis=1)
        out[0, p] = exchanged(whole, chip)
    for g in (g_row2, g_col1, g_row1, g_image1, g_green, g_col0, g_row0, g_image0):
        g.drain()
    for copy in tail:
        copy.wait_send()


def on_device(left_inverse, regions, region_mass, region_alpha, energy_grid, energy_index):
    count, _, rows, size = left_inverse.shape
    high, panel = SIDE * rows, SIDE * CORES * rows
    vmem = pl.BlockSpec(memory_space=pltpu.VMEM)
    smem = pl.BlockSpec(memory_space=pltpu.SMEM)
    copies = 4 * 6 + 4 * 14 + 3
    return pl.pallas_call(
        kernel,
        out_shape=jax.ShapeDtypeStruct((count - 1, 2, rows, size), F32),
        in_specs=[pl.BlockSpec(memory_space=pl.ANY), vmem, smem, smem, smem, smem],
        out_specs=vmem,
        scratch_shapes=[
            pltpu.VMEM((2, SIDE, rows, size), BF),
            pltpu.VMEM((2, SIDE, rows, size), BF),
            pltpu.VMEM((2, SIDE, rows, size), BF),
            pltpu.VMEM((2, SIDE, CORES, rows, size), BF),
            pltpu.VMEM((2, SIDE, CORES, rows, size), BF),
            pltpu.VMEM((2, panel, size), BF),
            pltpu.VMEM((2, rows, size), BF),
            pltpu.VMEM((2, SIDE, SIDE, CORES, rows, panel), BF),
            pltpu.VMEM((2, SIDE, SIDE, CORES, rows, panel), BF),
            pltpu.VMEM((2, SIDE, high, panel), BF),
            pltpu.VMEM((SIDE, 2, rows, panel), BF),
            pltpu.VMEM((SIDE, 2, rows, panel), BF),
            pltpu.VMEM((2, high, panel), F32),
            pltpu.VMEM((2, size, 128), F32),
            pltpu.VMEM((size, panel), BF),
            pltpu.SemaphoreType.DMA((copies,)),
            pltpu.SemaphoreType.DMA((copies,)),
            pltpu.SemaphoreType.DMA((8,)),
        ],
        compiler_params=pltpu.CompilerParams(
            collective_id=0, has_side_effects=True, vmem_limit_bytes=60 * 1024 * 1024
        ),
    )(left_inverse, regions, region_mass, region_alpha, energy_grid, energy_index)


def solution(mesh):
    in_specs = (P("energy", None, "cols", None), P(), P(), P(), P(), P("energy"))
    out_specs = P("energy", None, "cols", None)
    return jax.shard_map(
        on_device, mesh=mesh, in_specs=in_specs, out_specs=out_specs, check_vma=False
    )
```

```python
import jax
import jax.numpy as jnp
from jax import lax
from jax.experimental import pallas as pl
from jax.experimental.pallas import tpu as pltpu
from jax.sharding import PartitionSpec as P

SIDE = 4
CORES = 2
BF = jnp.bfloat16
F32 = jnp.float32


def dot(a, b):
    return lax.dot_general(a, b, (((1,), (0,)), ((), ())), preferred_element_type=F32)


def dot_t(a, b):
    return lax.dot_general(a, b, (((1,), (1,)), ((), ())), preferred_element_type=F32)


class Sems:
    def __init__(self, ref):
        self.ref = ref
        self.used = 0

    def take(self):
        self.used += 1
        return self.ref.at[self.used - 1]


class Remote:
    def __init__(self, copy):
        self.copy = copy
        self.left = False

    def wait_recv(self):
        self.copy.wait_recv()

    def wait_send(self):
        if not self.left:
            self.left = True
            self.copy.wait_send()


class Gather:
    def __init__(self, me, device, source, slot, send, recv, sibling=None, parts=1):
        self.me = me
        self.plus = lax.rem(me + 1, SIDE)
        self.minus = lax.rem(me + 3, SIDE)
        self.far = lax.rem(me + 2, SIDE)
        self.right, self.left = device(self.plus), device(self.minus)
        self.source, self.slot = source, slot
        self.send, self.recv = send, recv
        self.sibling = sibling
        self.parts = parts
        self.copies = []
        self.sib = {"own": [], "minus": [], "plus": [], "far": []}

    def remote(self, src, dst, device):
        copy = pltpu.make_async_remote_copy(
            src_ref=src,
            dst_ref=dst,
            send_sem=self.send.take(),
            recv_sem=self.recv.take(),
            device_id={"cols": device},
            device_id_type=pl.DeviceIdType.MESH,
        )
        copy.start()
        copy = Remote(copy)
        self.copies.append(copy)
        return copy

    def cut(self, ref, q):
        if self.parts == 1:
            return ref
        n = ref.shape[0] // self.parts
        return ref.at[q * n : (q + 1) * n]

    def first(self):
        self.r0 = self.remote(self.source(0), self.slot(self.me, 0), self.right)
        self.l1 = self.remote(self.source(1), self.slot(self.me, 1), self.left)

    def second(self):
        self.r1 = self.remote(self.source(1), self.slot(self.me, 1), self.right)
        self.l0 = self.remote(self.source(0), self.slot(self.me, 0), self.left)
        if self.sibling is not None:
            for p in range(2):
                self.share("own", self.source(p), self.slot(self.me, p))

    def sent(self):
        self.r0.wait_send()
        self.l1.wait_send()

    def share(self, name, src, dst):
        if self.sibling is not None:
            self.sib[name].append(self.remote(src, dst, self.sibling))

    def share_slot(self, name, ref):
        self.share(name, ref, ref)

    def forward(self):
        self.r0.wait_recv()
        ref = self.slot(self.minus, 0)
        self.fr = [self.remote(self.cut(ref, q), self.cut(ref, q), self.right) for q in range(self.parts)]
        self.l1.wait_recv()
        ref = self.slot(self.plus, 1)
        self.fl = [self.remote(self.cut(ref, q), self.cut(ref, q), self.left) for q in range(self.parts)]
        self.share_slot("minus", self.slot(self.minus, 0))
        self.share_slot("plus", self.slot(self.plus, 1))

    def passed_on(self):
        for copy in self.fr + self.fl:
            copy.wait_send()

    def near(self):
        self.r1.wait_recv()
        self.share_slot("minus", self.slot(self.minus, 1))
        self.l0.wait_recv()
        self.share_slot("plus", self.slot(self.plus, 0))

    def last(self):
        for q in range(self.parts):
            self.fr[q].wait_recv()
            self.share_slot("far", self.cut(self.slot(self.far, 0), q))
            self.fl[q].wait_recv()
            self.share_slot("far", self.cut(self.slot(self.far, 1), q))

    def sib_wait(self):
        for name in ("own", "minus", "plus", "far"):
            for copy in self.sib[name]:
                copy.wait_recv()

    def drain(self):
        for copy in self.copies:
            copy.wait_send()


def kernel(
    left,
    regions,
    region_mass,
    region_alpha,
    energy_grid,
    energy_index,
    out,
    row2,
    row1,
    row0,
    col1,
    col0,
    scaled1,
    scaled0,
    image1,
    image0,
    green,
    ends,
    final,
    acc,
    own1,
    hops,
    send_sems,
    recv_sems,
    local_sems,
    end_send,
    end_recv,
):
    me = lax.axis_index("cols")
    c = lax.rem(me, CORES)
    j = lax.rem(me // CORES, SIDE)
    i = me // (CORES * SIDE)
    sibling = me + 1 - 2 * c

    def along_x(x):
        return (x * SIDE + j) * CORES + c

    def along_y(y):
        return (i * SIDE + y) * CORES + c

    rows = left.shape[2]
    size = left.shape[3]
    panel = SIDE * CORES * rows
    half = 2 * rows
    here = pl.ds(pl.multiple_of(i * panel, 128), panel)

    def lanes(k):
        if isinstance(k, int):
            return slice(k * panel, (k + 1) * panel)
        return pl.ds(pl.multiple_of(k * panel, 128), panel)

    send, recv, local = Sems(send_sems), Sems(recv_sems), Sems(local_sems)

    barrier = pltpu.get_barrier_semaphore()
    peers = [sibling]
    peers += [along_x(lax.rem(i + s, SIDE)) for s in (1, 2, 3)]
    peers += [along_y(lax.rem(j + s, SIDE)) for s in (1, 3)]
    for peer in peers:
        pl.semaphore_signal(barrier, inc=1, device_id={"cols": peer}, device_id_type=pl.DeviceIdType.MESH)
    pl.semaphore_wait(barrier, len(peers))

    def rows_gather(s, row, parts):
        return Gather(j, along_y, lambda p: left.at[s, p], lambda m, p: row.at[p, m, c], send, recv, sibling, parts)

    def cols_gather(s, col):
        return Gather(i, along_x, lambda p: left.at[s, p], lambda k, p: col.at[p, k], send, recv)

    def image_gather(image, h):
        return Gather(i, along_x, lambda p: image.at[h, i, p], lambda k, p: image.at[h, k, p], send, recv)

    def green_gather(s):
        return Gather(
            j, along_y, lambda p: green.at[p, s, j, c], lambda m, p: green.at[p, s, m, c], send, recv, sibling
        )

    g_row2 = rows_gather(2, row2, 1)
    g_col1 = cols_gather(1, col1)
    g_row1 = rows_gather(1, row1, 1)
    g_col0 = cols_gather(0, col0)
    g_row0 = rows_gather(0, row0, 1)
    g_b = [image_gather(image1, h) for h in range(2)]
    g_c = [green_gather(s) for s in range(SIDE)]
    g_d = [image_gather(image0, s) for s in range(SIDE)]

    g_row2.first()
    g_col1.first()
    locals_ = {}
    for name, s, dst in (
        ("col1", 1, lambda p: col1.at[p, i]),
        ("row2", 2, lambda p: row2.at[p, j, c]),
        ("row1", 1, lambda p: row1.at[p, j, c]),
        ("col0", 0, lambda p: col0.at[p, i]),
        ("row0", 0, lambda p: row0.at[p, j, c]),
    ):
        locals_[name] = []
        for p in range(2):
            copy = pltpu.make_async_copy(left.at[s, p], dst(p), local.take())
            copy.start()
            locals_[name].append(copy)

    def local_wait(name):
        for copy in locals_[name]:
            copy.wait()

    level = jnp.float32(0.0)
    wanted = energy_index[0]
    for e in range(energy_grid.shape[0]):
        level = jnp.where(wanted == e, energy_grid[e], level)
    where = regions[...]
    mass = jnp.zeros(where.shape, F32)
    for r in range(region_mass.shape[0]):
        mass = jnp.where(where == r, region_mass[r] * (1.0 + region_alpha[r] * level), mass)
    hops[0:1] = 2.0 / (mass[0:1] + mass[1:2])
    hops[1:2] = 2.0 / (mass[1:2] + mass[2:3])

    def scale1(k):
        first = pl.multiple_of(lax.rem(k, 2) * rows, 16)
        for p in range(2):
            scaled1[k // 2, p, pl.ds(first, rows), :] = (col1[p, k].astype(F32) * hops[1:2]).astype(BF)

    def scale0(k):
        first = pl.multiple_of(k * rows, 16)
        for p in range(2):
            scaled0[p, pl.ds(first, rows), :] = (col0[p, k].astype(F32) * hops[0:1]).astype(BF)

    def whole(row, p):
        return row[p].reshape(panel, size)

    def chunk(row, p, k):
        return row[p, :, :, :, lanes(k)].reshape(panel, panel)

    g_row2.sent()
    g_row2.second()
    g_col1.sent()
    g_col1.second()
    local_wait("col1")
    scale1(i)
    g_row2.forward()
    g_col1.forward()
    g_row2.near()
    g_col1.near()
    g_row2.passed_on()
    g_row1.first()
    g_col1.passed_on()
    g_col0.first()
    scale1(g_col1.minus)
    scale1(g_col1.plus)
    local_wait("row2")
    g_row2.last()
    g_col1.last()
    scale1(g_col1.far)
    g_row1.sent()
    g_row1.second()
    g_row2.sib_wait()

    def first_image(h):
        a = scaled1[h].reshape(2 * half, size)
        re, im = dot_t(a, whole(row2, 0)), dot_t(a, whole(row2, 1))
        hop = hops[1:2, here]
        image1[h, i, 0] = (hop * (re[:half] - im[half:])).astype(BF)
        image1[h, i, 1] = (hop * (im[:half] + re[half:])).astype(BF)

    first_image(0)
    g_b[0].first()
    g_row1.forward()
    first_image(1)
    g_b[1].first()

    def add(image, row, h, k, start, count, init):
        a = image[h, k].reshape(2 * count, panel)
        for p in range(2):
            value = dot_t(a, chunk(row, p, k))
            if init:
                acc[p, start : start + 2 * count, :] = value
            else:
                acc[p, start : start + 2 * count, :] += value

    def planes(start, count):
        re, im = acc[0, start : start + 2 * count, :], acc[1, start : start + 2 * count, :]
        return re[:count] - im[count:], im[:count] + re[count:]

    g_row1.near()
    for h in range(2):
        g_b[h].sent()
        g_b[h].second()
    g_row1.passed_on()
    g_row0.first()
    for h in range(2):
        g_b[h].forward()
    local_wait("row1")
    g_row1.last()
    g_b[0].near()
    g_row1.sib_wait()
    for h in range(2):
        if h:
            g_b[h].near()
        start = h * 2 * half
        add(image1, row1, h, i, start, half, True)
        add(image1, row1, h, g_b[h].minus, start, half, False)
        add(image1, row1, h, g_b[h].plus, start, half, False)
        g_b[h].last()
        add(image1, row1, h, g_b[h].far, start, half, False)
        values = planes(start, half)
        for t in range(2):
            k = 2 * h + t
            for p in range(2):
                value = col1[p, k, :, here].astype(F32) + values[p][t * rows : (t + 1) * rows]
                green[p, k, j, c] = value.astype(BF)
                own1[p, k * rows : (k + 1) * rows, :] = value
            g_c[k].first()

    g_col0.second()
    g_col0.forward()
    local_wait("col0")
    scale0(i)
    for s in range(SIDE):
        g_c[s].sent()
        g_c[s].second()
    for s in range(SIDE):
        g_c[s].forward()
    g_col0.near()
    scale0(g_col0.minus)
    scale0(g_col0.plus)
    for s in range(SIDE):
        g_c[s].near()
    g_col0.last()
    scale0(g_col0.far)
    for s in range(SIDE):
        g_c[s].passed_on()
    g_row0.second()
    g_row0.forward()
    for s in range(SIDE):
        g_c[s].last()
    for s in range(SIDE):
        g_c[s].sib_wait()
        a = scaled0[:, :, lanes(s)].reshape(2 * SIDE * rows, panel)
        for p in range(2):
            value = dot(a, green[p, s].reshape(panel, panel))
            if s:
                acc[p] += value
            else:
                acc[p] = value
    high = SIDE * rows
    hop = hops[0:1, here]
    for s in range(SIDE):
        a, b = slice(s * rows, (s + 1) * rows), slice(high + s * rows, high + (s + 1) * rows)
        image0[s, i, 0] = (hop * (acc[0, a, :] - acc[1, b, :])).astype(BF)
        image0[s, i, 1] = (hop * (acc[1, a, :] + acc[0, b, :])).astype(BF)
        g_d[s].first()

    r = lax.broadcasted_iota(jnp.int32, (rows, panel), 0)
    q = lax.broadcasted_iota(jnp.int32, (rows, panel), 1)
    pick = jnp.where(q == r + (j * CORES + c) * rows, 1.0, 0.0).astype(BF)
    mine = pl.ds(pl.multiple_of(i * rows, 8), rows)
    for p in range(2):
        for k in range(SIDE):
            out[1, p, :, lanes(k)] = dot_t(pick, green[p, k].reshape(panel, panel))
        out[1, p, :, here] = own1[p, mine, :]
    for s in range(SIDE):
        g_d[s].sent()
        g_d[s].second()
    for s in range(SIDE):
        g_d[s].forward()
    g_row0.near()
    local_wait("row0")
    g_row0.last()
    g_row0.sib_wait()
    for s in range(SIDE):
        start = s * 2 * rows
        add(image0, row0, s, i, start, rows, True)
        g_d[s].near()
        add(image0, row0, s, g_d[s].minus, start, rows, False)
        add(image0, row0, s, g_d[s].plus, start, rows, False)

    def end(s, d):
        return pltpu.make_async_remote_copy(
            src_ref=ends.at[s],
            dst_ref=final.at[i],
            send_sem=end_send.at[d],
            recv_sem=end_recv.at[d],
            device_id={"cols": along_x(s)},
            device_id_type=pl.DeviceIdType.MESH,
        )

    for s in range(SIDE):
        start = s * 2 * rows
        g_d[s].last()
        add(image0, row0, s, g_d[s].far, start, rows, False)
        values = planes(start, rows)
        for p in range(2):
            value = col0[p, s, :, here].astype(F32) + values[p]
            ends[s, p] = value.astype(BF)
            own1[p, s * rows : (s + 1) * rows, :] = value

        @pl.when(i != s)
        def _():
            end(s, lax.rem(s - i + SIDE, SIDE)).start()

    final[i] = ends[i]
    for d in range(1, SIDE):
        end(lax.rem(i + d, SIDE), d).wait_recv()
    for p in range(2):
        for k in range(SIDE):
            out[0, p, :, lanes(k)] = final[k, p].astype(F32)
        out[0, p, :, here] = own1[p, mine, :]
    for g in [g_row2, g_col1, g_row1, g_col0, g_row0] + g_b + g_c + g_d:
        g.drain()
    for d in range(1, SIDE):
        end(lax.rem(i + d, SIDE), d).wait_send()


def on_device(left_inverse, regions, region_mass, region_alpha, energy_grid, energy_index):
    arrays = (left_inverse, regions, region_mass, region_alpha, energy_grid, energy_index)
    count, _, rows, size = left_inverse.shape
    panel = SIDE * CORES * rows
    vmem = pl.BlockSpec(memory_space=pltpu.VMEM)
    smem = pl.BlockSpec(memory_space=pltpu.SMEM)
    copies = 3 * 14 + 2 * 6 + 2 * 6 + 4 * 14 + 4 * 6
    return pl.pallas_call(
        kernel,
        out_shape=jax.ShapeDtypeStruct((count - 1, 2, rows, size), F32),
        in_specs=[pl.BlockSpec(memory_space=pl.ANY), vmem, smem, smem, smem, smem],
        out_specs=vmem,
        scratch_shapes=[
            pltpu.VMEM((2, SIDE, CORES, rows, size), BF),
            pltpu.VMEM((2, SIDE, CORES, rows, size), BF),
            pltpu.VMEM((2, SIDE, CORES, rows, size), BF),
            pltpu.VMEM((2, SIDE, rows, size), BF),
            pltpu.VMEM((2, SIDE, rows, size), BF),
            pltpu.VMEM((2, 2, 2 * rows, size), BF),
            pltpu.VMEM((2, SIDE * rows, size), BF),
            pltpu.VMEM((2, SIDE, 2, 2 * rows, panel), BF),
            pltpu.VMEM((SIDE, SIDE, 2, rows, panel), BF),
            pltpu.VMEM((2, SIDE, SIDE, CORES, rows, panel), BF),
            pltpu.VMEM((SIDE, 2, rows, panel), BF),
            pltpu.VMEM((SIDE, 2, rows, panel), BF),
            pltpu.VMEM((2, panel, panel), F32),
            pltpu.VMEM((2, SIDE * rows, panel), F32),
            pltpu.VMEM((2, size), F32),
            pltpu.SemaphoreType.DMA((copies,)),
            pltpu.SemaphoreType.DMA((copies,)),
            pltpu.SemaphoreType.DMA((10,)),
            pltpu.SemaphoreType.DMA((SIDE,)),
            pltpu.SemaphoreType.DMA((SIDE,)),
        ],
        compiler_params=pltpu.CompilerParams(
            collective_id=0, has_side_effects=True, vmem_limit_bytes=40 * 1024 * 1024
        ),
    )(*(pltpu.with_memory_space_constraint(x, pltpu.HBM) for x in arrays[:5]), energy_index)


def solution(mesh):
    in_specs = (P("energy", None, "cols", None), P(), P(), P(), P(), P("energy"))
    out_specs = P("energy", None, "cols", None)
    return jax.shard_map(
        on_device, mesh=mesh, in_specs=in_specs, out_specs=out_specs, check_vma=False
    )
```

```python
import functools

import jax
import jax.numpy as jnp
from jax import lax
from jax.experimental import pallas as pl
from jax.experimental.pallas import tpu as pltpu
from jax.sharding import PartitionSpec as P

SIDE = 4
CORES = 2
BF = jnp.bfloat16
F32 = jnp.float32


def dot(a, b):
    return lax.dot_general(a, b, (((1,), (0,)), ((), ())), preferred_element_type=F32)


def dot_t(a, b):
    return lax.dot_general(a, b, (((1,), (1,)), ((), ())), preferred_element_type=F32)


def complex_dot(ar, ai, br, bi, op):
    return op(ar, br) - op(ai, bi), op(ar, bi) + op(ai, br)


class Sems:
    def __init__(self, ref):
        self.ref = ref
        self.used = 0

    def take(self):
        self.used += 1
        return self.ref.at[self.used - 1]


class Gather:
    def __init__(self, me, device, source, slot, send, recv, sibling=None):
        self.me = me
        self.plus = lax.rem(me + 1, SIDE)
        self.minus = lax.rem(me + 3, SIDE)
        self.far = lax.rem(me + 2, SIDE)
        self.device, self.source, self.slot = device, source, slot
        self.send, self.recv = send, recv
        self.sibling = sibling
        self.copies = []
        self.sib = {}

    def remote(self, src, dst, device):
        copy = pltpu.make_async_remote_copy(
            src_ref=src,
            dst_ref=dst,
            send_sem=self.send.take(),
            recv_sem=self.recv.take(),
            device_id={"cols": device},
            device_id_type=pl.DeviceIdType.MESH,
        )
        copy.start()
        self.copies.append(copy)
        return copy

    def start(self):
        right, left = self.device(self.plus), self.device(self.minus)
        me = self.me
        self.r0 = self.remote(self.source(0), self.slot(me, 0), right)
        self.l1 = self.remote(self.source(1), self.slot(me, 1), left)
        self.r1 = self.remote(self.source(1), self.slot(me, 1), right)
        self.l0 = self.remote(self.source(0), self.slot(me, 0), left)
        if self.sibling is not None:
            for p in range(2):
                self.share("own", me, p, self.source(p))

    def share(self, name, slot, p, src=None):
        if self.sibling is None:
            return
        ref = self.slot(slot, p)
        self.sib[name, p] = self.remote(ref if src is None else src, ref, self.sibling)

    def forward(self):
        self.r0.wait_recv()
        self.fr = self.remote(self.slot(self.minus, 0), self.slot(self.minus, 0), self.device(self.plus))
        self.l1.wait_recv()
        self.fl = self.remote(self.slot(self.plus, 1), self.slot(self.plus, 1), self.device(self.minus))
        self.share("minus", self.minus, 0)
        self.share("plus", self.plus, 1)

    def near(self):
        self.r1.wait_recv()
        self.share("minus", self.minus, 1)
        self.l0.wait_recv()
        self.share("plus", self.plus, 0)

    def last(self):
        self.fr.wait_recv()
        self.share("far", self.far, 0)
        self.fl.wait_recv()
        self.share("far", self.far, 1)

    def sib_wait(self, name):
        if self.sibling is not None:
            for p in range(2):
                self.sib[name, p].wait_recv()

    def drain(self):
        for copy in self.copies:
            copy.wait_send()


def group_order(pieces):
    return jnp.concatenate([pieces[b][a] for a in range(SIDE) for b in range(SIDE)], axis=-1)


def exchanged(value, width):
    rows = [
        [value[:, (a * SIDE + b) * width : (a * SIDE + b + 1) * width] for b in range(SIDE)] for a in range(SIDE)
    ]
    return group_order(rows)


def kernel(
    left,
    regions_in,
    region_mass_in,
    region_alpha_in,
    energy_grid_in,
    energy_index,
    out,
    row2,
    row1,
    row0,
    col1,
    col0,
    scaled,
    mine0,
    image1,
    image0,
    green1,
    final,
    ends,
    acc,
    hop_t,
    pick,
    send_sems,
    recv_sems,
    local_sems,
    own1,
    regions,
    region_mass,
    region_alpha,
    energy_grid,
    small_sems,
):
    me = lax.axis_index("cols")
    c = lax.rem(me, CORES)
    j = lax.rem(me // CORES, SIDE)
    i = me // (CORES * SIDE)
    sibling = me + 1 - 2 * c

    def at(x, y):
        return (x * SIDE + y) * CORES + c

    def along_x(x):
        return at(x, j)

    def along_y(y):
        return at(i, y)

    rows = left.shape[2]
    size = left.shape[3]
    chip = CORES * rows
    panel = SIDE * chip
    high = SIDE * rows

    send, recv, local = Sems(send_sems), Sems(recv_sems), Sems(local_sems)

    barrier = pltpu.get_barrier_semaphore()
    peers = [sibling] + [along_x(lax.rem(i + s, SIDE)) for s in (1, 3)] + [along_y(lax.rem(j + s, SIDE)) for s in (1, 2, 3)]
    for peer in peers:
        pl.semaphore_signal(barrier, inc=1, device_id={"cols": peer}, device_id_type=pl.DeviceIdType.MESH)
    small = []
    for src, dst in (
        (regions_in, regions),
        (region_mass_in, region_mass),
        (region_alpha_in, region_alpha),
        (energy_grid_in, energy_grid),
    ):
        small.append(pltpu.make_async_copy(src, dst, small_sems.at[len(small)]))
        small[-1].start()
    pl.semaphore_wait(barrier, len(peers))

    g_row2 = Gather(j, along_y, lambda p: left.at[2, p], lambda s, p: row2.at[p, s], send, recv)
    g_col1 = Gather(i, along_x, lambda p: left.at[1, p], lambda s, p: col1.at[p, s, c], send, recv, sibling)
    g_row1 = Gather(j, along_y, lambda p: left.at[1, p], lambda s, p: row1.at[p, s], send, recv)
    g_image1 = Gather(
        i, along_x, lambda p: image1.at[p, i, :, c], lambda s, p: image1.at[p, s, :, c], send, recv, sibling
    )
    g_green = Gather(j, along_y, lambda p: green1.at[p, j], lambda s, p: green1.at[p, s], send, recv)
    g_col0 = Gather(i, along_x, lambda p: mine0.at[p], lambda s, p: col0.at[p, s, c], send, recv, sibling)
    g_row0 = Gather(j, along_y, lambda p: left.at[0, p], lambda s, p: row0.at[p, s], send, recv)
    g_image0 = Gather(
        i, along_x, lambda p: image0.at[p, i, :, c], lambda s, p: image0.at[p, s, :, c], send, recv, sibling
    )

    g_row2.start()
    g_col1.start()
    locals_ = {}
    for name, src, dst in (
        ("row2", 2, lambda p: row2.at[p, j]),
        ("col1", 1, lambda p: col1.at[p, i, c]),
        ("row1", 1, lambda p: row1.at[p, j]),
        ("row0", 0, lambda p: row0.at[p, j]),
    ):
        locals_[name] = []
        for p in range(2):
            copy = pltpu.make_async_copy(left.at[src, p], dst(p), local.take())
            copy.start()
            locals_[name].append(copy)

    def local_wait(name):
        for copy in locals_[name]:
            copy.wait()

    for copy in small:
        copy.wait()
    level = jnp.float32(0.0)
    wanted = energy_index[0]
    for e in range(energy_grid.shape[0]):
        level = jnp.where(wanted == e, energy_grid[e], level)
    where = regions[...]
    mass = jnp.zeros(where.shape, F32)
    for r in range(region_mass.shape[0]):
        mass = jnp.where(where == r, region_mass[r] * (1.0 + region_alpha[r] * level), mass)
    hop0 = 2.0 / (mass[0:1] + mass[1:2])
    hop1 = 2.0 / (mass[1:2] + mass[2:3])
    for s, hop in enumerate((hop0, hop1)):
        for b in range(size // 128):
            tile = jnp.broadcast_to(hop[:, b * 128 : (b + 1) * 128], (128, 128))
            hop_t[s, b * 128 : (b + 1) * 128, :] = tile.T
    hop0_c = exchanged(hop0, chip)

    local_wait("row0")
    for p in range(2):
        mine0[p] = exchanged(row0[p, j].astype(F32), chip).astype(BF)

    for k in range(SIDE):
        n = lax.broadcasted_iota(jnp.int32, (panel, panel), 0)
        q = lax.broadcasted_iota(jnp.int32, (panel, panel), 1)
        keep = n + (k - j) * chip == q
        keep = keep & (q >= k * chip) & (q < (k + 1) * chip)
        pick[k * panel : (k + 1) * panel, :] = jnp.where(keep, 1.0, 0.0).astype(BF)

    def scale_block(col, slot, core, hop):
        for p in range(2):
            start = pl.multiple_of((slot * CORES + core) * rows, 16)
            scaled[p, pl.ds(start, rows), :] = (col[p, slot, core].astype(F32) * hop).astype(BF)

    def scale_own(col, slot, hop):
        scale_block(col, slot, c, hop)

    def scale_sib(g, name, col, slot, hop):
        g.sib_wait(name)
        scale_block(col, slot, 1 - c, hop)

    def store_image(image, s, real, imag):
        for m in range(SIDE):
            start = pl.multiple_of(i * panel + m * chip + c * rows, 16)
            h = hop_t[s, pl.ds(start, rows), :]
            h = jnp.concatenate([h] * (panel // 128), axis=1)
            part = slice(m * rows, (m + 1) * rows)
            image[0, i, m, c] = (h * real[part]).astype(BF)
            image[1, i, m, c] = (h * imag[part]).astype(BF)

    def init_acc(row):
        for p in range(2):
            acc[p] = dot(row[p].reshape(high, size), pick[...])

    def add_chunk(row, image, k):
        lanes = pl.ds(pl.multiple_of(k * panel, 128), panel)
        ar, ai = (row[p, :, :, lanes].reshape(high, panel) for p in range(2))
        br, bi = (image[p, k].reshape(panel, panel) for p in range(2))
        real, imag = complex_dot(ar, ai, br, bi, dot)
        acc[0] += real
        acc[1] += imag

    g_row2.forward()
    g_col1.forward()
    g_row1.start()
    local_wait("col1")
    scale_own(col1, i, hop1)
    scale_sib(g_col1, "own", col1, i, hop1)
    g_col1.near()
    g_row2.near()
    scale_own(col1, g_col1.minus, hop1)
    scale_own(col1, g_col1.plus, hop1)
    scale_sib(g_col1, "minus", col1, g_col1.minus, hop1)
    scale_sib(g_col1, "plus", col1, g_col1.plus, hop1)
    local_wait("row2")
    g_col1.last()
    g_row2.last()
    scale_own(col1, g_col1.far, hop1)
    scale_sib(g_col1, "far", col1, g_col1.far, hop1)

    ar, ai = (row2[p].reshape(high, size) for p in range(2))
    real, imag = complex_dot(ar, ai, scaled[0], scaled[1], dot_t)
    store_image(image1, 1, real, imag)
    g_image1.start()

    g_row1.forward()
    local_wait("row1")
    g_row1.near()
    g_image1.forward()
    g_col0.start()
    g_image1.near()
    g_row1.last()
    init_acc(row1)
    g_image1.sib_wait("own")
    add_chunk(row1, image1, i)
    for name, slot in (("minus", g_image1.minus), ("plus", g_image1.plus)):
        g_image1.sib_wait(name)
        add_chunk(row1, image1, slot)
    g_image1.last()
    g_image1.sib_wait("far")
    add_chunk(row1, image1, g_image1.far)
    mine = pl.ds(pl.multiple_of(j * rows, 16), rows)
    for p in range(2):
        green1[p, j] = acc[p].astype(BF)
    g_green.start()
    for p in range(2):
        own1[p] = acc[p, mine, :]

    g_col0.forward()
    g_col0.near()
    g_green.forward()
    g_row0.start()

    def scale_col0(name, slot):
        if name != "own":
            scale_own(col0, slot, hop0_c)
        scale_sib(g_col0, name, col0, slot, hop0_c)

    for p in range(2):
        start = pl.multiple_of((i * CORES + c) * rows, 16)
        scaled[p, pl.ds(start, rows), :] = (mine0[p].astype(F32) * hop0_c).astype(BF)
    scale_col0("own", i)
    scale_col0("minus", g_col0.minus)
    scale_col0("plus", g_col0.plus)
    g_col0.last()
    scale_col0("far", g_col0.far)

    def green_chunk(m, first=False):
        lanes = pl.ds(pl.multiple_of(m * panel, 128), panel)
        real, imag = complex_dot(green1[0, m], green1[1, m], scaled[0, :, lanes], scaled[1, :, lanes], dot_t)
        if first:
            acc[0] = real
            acc[1] = imag
        else:
            acc[0] += real
            acc[1] += imag

    green_chunk(j, True)
    g_green.near()
    green_chunk(g_green.minus)
    green_chunk(g_green.plus)
    g_green.last()
    green_chunk(g_green.far)
    store_image(image0, 0, acc[0], acc[1])
    g_image0.start()

    g_row0.forward()
    for p in range(2):
        parts = [jnp.where(j == m, own1[p], green1[p, m, mine, :].astype(F32)) for m in range(SIDE)]
        whole = jnp.concatenate(parts, axis=1)
        out[1, p] = exchanged(whole, chip)
    g_row0.near()
    g_image0.forward()
    g_image0.near()
    g_row0.last()
    init_acc(row0)
    g_image0.sib_wait("own")
    add_chunk(row0, image0, i)
    for name, slot in (("minus", g_image0.minus), ("plus", g_image0.plus)):
        g_image0.sib_wait(name)
        add_chunk(row0, image0, slot)
    g_image0.last()
    g_image0.sib_wait("far")
    add_chunk(row0, image0, g_image0.far)

    for m in range(SIDE):
        for p in range(2):
            ends[m, p] = acc[p, m * rows : (m + 1) * rows, :].astype(BF)
    tail = []
    for shift in (2, 1, 3):
        to = lax.rem(j + shift, SIDE)
        copy = pltpu.make_async_remote_copy(
            src_ref=ends.at[to],
            dst_ref=final.at[j],
            send_sem=send.take(),
            recv_sem=recv.take(),
            device_id={"cols": along_y(to)},
            device_id_type=pl.DeviceIdType.MESH,
        )
        copy.start()
        tail.append(copy)
    final[j] = ends[j]
    for copy in tail:
        copy.wait_recv()
    for p in range(2):
        own0 = acc[p, mine, :]
        parts = [jnp.where(j == m, own0, final[m, p].astype(F32)) for m in range(SIDE)]
        whole = jnp.concatenate(parts, axis=1)
        out[0, p] = exchanged(whole, chip)
    for g in (g_row2, g_col1, g_row1, g_image1, g_green, g_col0, g_row0, g_image0):
        g.drain()
    for copy in tail:
        copy.wait_send()


def on_device(left_inverse, regions, region_mass, region_alpha, energy_grid, energy_index):
    arrays = (left_inverse, regions, region_mass, region_alpha, energy_grid)
    count, _, rows, size = left_inverse.shape
    high, panel = SIDE * rows, SIDE * CORES * rows
    vmem = pl.BlockSpec(memory_space=pltpu.VMEM)
    smem = pl.BlockSpec(memory_space=pltpu.SMEM)
    copies = 4 * 6 + 4 * 14 + 3
    return pl.pallas_call(
        kernel,
        out_shape=jax.ShapeDtypeStruct((count - 1, 2, rows, size), F32),
        in_specs=[pl.BlockSpec(memory_space=pl.ANY)] * 5 + [smem],
        out_specs=vmem,
        scratch_shapes=[
            pltpu.VMEM((2, SIDE, rows, size), BF),
            pltpu.VMEM((2, SIDE, rows, size), BF),
            pltpu.VMEM((2, SIDE, rows, size), BF),
            pltpu.VMEM((2, SIDE, CORES, rows, size), BF),
            pltpu.VMEM((2, SIDE, CORES, rows, size), BF),
            pltpu.VMEM((2, panel, size), BF),
            pltpu.VMEM((2, rows, size), BF),
            pltpu.VMEM((2, SIDE, SIDE, CORES, rows, panel), BF),
            pltpu.VMEM((2, SIDE, SIDE, CORES, rows, panel), BF),
            pltpu.VMEM((2, SIDE, high, panel), BF),
            pltpu.VMEM((SIDE, 2, rows, panel), BF),
            pltpu.VMEM((SIDE, 2, rows, panel), BF),
            pltpu.VMEM((2, high, panel), F32),
            pltpu.VMEM((2, size, 128), F32),
            pltpu.VMEM((size, panel), BF),
            pltpu.SemaphoreType.DMA((copies,)),
            pltpu.SemaphoreType.DMA((copies,)),
            pltpu.SemaphoreType.DMA((8,)),
            pltpu.VMEM((2, rows, panel), F32),
            pltpu.VMEM(regions.shape, jnp.int32),
            pltpu.SMEM(region_mass.shape, F32),
            pltpu.SMEM(region_alpha.shape, F32),
            pltpu.SMEM(energy_grid.shape, F32),
            pltpu.SemaphoreType.DMA((4,)),
        ],
        compiler_params=pltpu.CompilerParams(
            collective_id=0, has_side_effects=True, vmem_limit_bytes=44 * 1024 * 1024
        ),
    )(*(pltpu.with_memory_space_constraint(x, pltpu.HBM) for x in arrays), energy_index)


def solution(mesh):
    in_specs = (P("energy", None, "cols", None), P(), P(), P(), P(), P("energy"))
    out_specs = P("energy", None, "cols", None)
    return jax.shard_map(
        on_device, mesh=mesh, in_specs=in_specs, out_specs=out_specs, check_vma=False
    )
```
